32 devices in a mesh: vol: 4 (over y, core), ctl: 8 (over z, x).
Axes of the slice: x: 2, y: 2, z: 4, core: 2. Of those that a mesh axis runs over, the one named last changes fastest.
Arguments:
- vol_coords: bfloat16 [3, 8192], P(None, ('vol', 'ctl')), may hold values from 0 to 1
- vol_cotangent: bfloat16 [48, 8192], P(None, ('vol', 'ctl')), may hold values from -0.59765625 to 0.59765625
- ctl_coords: bfloat16 [3, 8192], P(None, ('ctl', 'vol')), may hold values from 0 to 1
- ctl_weights: bfloat16 [48, 8192], P(None, ('ctl', 'vol')), may hold values from -0.029907227 to 0.029907227
Outputs:
- weight_grad: float32 [48, 8192], P(None, ('ctl', 'vol'))
- vol_coord_grad: float32 [3, 8192], P(None, ('vol', 'ctl'))
- ctl_coord_grad: float32 [3, 8192], P(None, ('ctl', 'vol'))
The draws below stay inside these ranges and needn't reach their ends.
All inputs are finite; a program needn't handle non-finite values.
Results may differ from the reference program's by a relative error of at most 0.0028.
Values may be sent and summed in bfloat16 or wider, within the bound.
A program may use at most 64 MiB of HBM per device.

```python
import math
import jax
import jax.numpy as jnp
from jax import lax

ROWS = 48
NVOL = 8192
NCTL = 8192


def level_of(own_key, shape, shards, low, top_value):
    loudness = 1.0
    for dim, shards_of in shards:
        steps = jax.random.uniform(jax.random.fold_in(jax.random.fold_in(own_key, 6), dim), (shards_of,), jnp.float32, low / len(shards), top_value / len(shards))
        loudness = loudness * jnp.repeat(jnp.exp(steps), shape[dim] // shards_of).reshape((-1,) + (1,) * (len(shape) - 1 - dim))
    return loudness


def noise(own_key, dims, spread, most, shards=(), held_as=jnp.bfloat16):
    result = jax.random.normal(own_key, dims, jnp.float32) * spread
    if len(shards) > 0:
        result = level_of(own_key, dims, shards, -0.22, 0.18) * result
    return jnp.clip(result, min=-most, max=most).astype(held_as)


def setup_inputs(seed: int = 0) -> dict:
    splits = jax.random.split(jax.random.key(seed), 5)
    return {
        "vol_coords": jnp.clip(1.0 * jax.random.uniform(splits[0], (3, NVOL), jnp.float32) ** level_of(splits[0], (3, NVOL), ((1, 32),), -0.2, 0.2), 0.0, 1.0).astype(jnp.bfloat16),
        "vol_cotangent": noise(splits[1], (ROWS, NVOL), 0.1, 0.59765625, ((1, 32),)),
        "ctl_coords": jnp.clip(1.0 * jax.random.uniform(splits[2], (3, NCTL), jnp.float32) ** level_of(splits[2], (3, NCTL), ((1, 32),), -0.2, 0.2), 0.0, 1.0).astype(jnp.bfloat16),
        "ctl_weights": noise(splits[3], (ROWS, NCTL), 0.005, 0.029907227, ((1, 32),)),
    }


support_radius = 0.25
slope_factor = -20.0 / (0.25 * 0.25)

def tile_terms(vol_xyz, vol_cot, ctl_xyz, ctl_wts):
    vol_pos = vol_xyz.astype(jnp.float32)
    ctl_pos = ctl_xyz.astype(jnp.float32)
    squared = jnp.zeros((vol_pos.shape[1], ctl_pos.shape[1]), jnp.float32)
    for component in range(3):
        offset = vol_pos[component][:, None] - ctl_pos[component][None, :]
        squared = squared + offset * offset
    ratio = jnp.sqrt(squared) / support_radius
    inside = jnp.maximum(1.0 - ratio, 0.0)
    cubic_term = inside * inside * inside
    kernel = (cubic_term * inside * (4.0 * ratio + 1.0)).astype(jnp.bfloat16)
    pair_dot = lax.dot_general(vol_cot, ctl_wts, (((0,), (0,)), ((), ())), preferred_element_type=jnp.float32)
    weighting = slope_factor * cubic_term * pair_dot
    weight_grad = jnp.dot(vol_cot, kernel, preferred_element_type=jnp.float32)
    row_total = lax.optimization_barrier(jnp.sum(weighting, axis=1))
    col_total = lax.optimization_barrier(jnp.sum(weighting, axis=0))
    pulled = lax.dot_general(ctl_pos, weighting, (((1,), (1,)), ((), ())), precision=lax.Precision.HIGHEST, preferred_element_type=jnp.float32)
    pushed = jnp.dot(vol_pos, weighting, precision=lax.Precision.HIGHEST, preferred_element_type=jnp.float32)
    vol_grad = vol_pos * row_total[None, :] - pulled
    ctl_grad = ctl_pos * col_total[None, :] - pushed
    return (vol_grad, weight_grad, ctl_grad)

def sweep(vol_xyz, vol_cot, ctl_xyz, ctl_wts, limit):
    vol_count = vol_xyz.shape[1]
    ctl_count = ctl_xyz.shape[1]
    block_len = math.gcd(vol_count, limit)
    blocks = vol_count // block_len
    stacked_xyz = vol_xyz.reshape(3, blocks, block_len).transpose(1, 0, 2)
    stacked_cot = vol_cot.reshape(vol_cot.shape[0], blocks, block_len).transpose(1, 0, 2)

    def advance(carry, items):
        xyz_block, cot_block = items
        vol_grad, weight_grad, ctl_grad = tile_terms(xyz_block, cot_block, ctl_xyz, ctl_wts)
        return ((carry[0] + weight_grad, carry[1] + ctl_grad), vol_grad)
    start_carry = (jnp.zeros((vol_cot.shape[0], ctl_count), jnp.float32), jnp.zeros((3, ctl_count), jnp.float32))
    totals, vol_parts = lax.scan(advance, start_carry, (stacked_xyz, stacked_cot))
    vol_grad = vol_parts.transpose(1, 0, 2).reshape(3, vol_count)
    return (vol_grad, totals[0], totals[1])

def reference(vol_coords, vol_cotangent, ctl_coords, ctl_weights):
    vol_grad, weight_grad, ctl_grad = sweep(vol_coords, vol_cotangent, ctl_coords, ctl_weights, 1024)
    return (weight_grad, vol_grad, ctl_grad)
```

```python
import functools
import math

import jax
import jax.numpy as jnp
from jax import lax
from jax.experimental import pallas as pl
from jax.experimental.pallas import tpu as pltpu
from jax.sharding import PartitionSpec as P

MESH = pl.DeviceIdType.MESH
slope_factor = -20.0 / (0.25 * 0.25)
inverse_square = 16.0
AUG = 16


def augment(dst, coords_ref, values_ref, norm_row, ones_row):
    rows = values_ref.shape[0]
    dst[0, :rows] = values_ref[...]
    pos = coords_ref[...].astype(jnp.float32)
    x, y, z = pos[0:1], pos[1:2], pos[2:3]
    norm = inverse_square * (x * x + y * y + z * z)
    high = norm.astype(jnp.bfloat16).astype(jnp.float32)
    rest = norm - high
    middle = rest.astype(jnp.bfloat16).astype(jnp.float32)
    low = rest - middle
    row = lax.broadcasted_iota(jnp.int32, (AUG, pos.shape[1]), 0)
    aug = jnp.where((row >= ones_row) & (row < ones_row + 3), 1.0, 0.0)
    pieces = ((0, x), (1, y), (2, z), (norm_row, high), (norm_row + 1, middle), (norm_row + 2, low))
    for at, piece in pieces:
        aug = jnp.where(row == at, piece, aug)
    dst[0, rows:] = aug.astype(jnp.bfloat16)


def kernel(
    nv, nc, vxyz, vcot, cxyz, cwts, out_w, out_v, out_c,
    vpack, cpack, vt, rhs, wacc, cacc, wsend, wrecv, psend, precv,
    vs_sem, vr_sem, cs_sem, cr_sem, ws_sem, wr_sem, ps_sem, pr_sem,
):
    rows, own_v = vcot.shape
    own_c = cwts.shape[1]
    my_v, my_c = lax.axis_index("vol"), lax.axis_index("ctl")
    barrier = pltpu.get_barrier_semaphore()
    for s in range(1, nv):
        pl.semaphore_signal(barrier, inc=1, device_id={"vol": lax.rem(my_v + s, nv)}, device_id_type=MESH)
    for t in range(1, nc):
        pl.semaphore_signal(barrier, inc=1, device_id={"ctl": lax.rem(my_c + t, nc)}, device_id_type=MESH)

    augment(vpack, vxyz, vcot, 3, 6)
    augment(cpack, cxyz, cwts, 6, 3)
    pl.semaphore_wait(barrier, nv + nc - 2)

    def ctl_copy(s):
        return pltpu.make_async_remote_copy(
            src_ref=cpack.at[0], dst_ref=cpack.at[s], send_sem=cs_sem.at[s], recv_sem=cr_sem.at[s],
            device_id={"vol": lax.rem(my_v + nv - s, nv)}, device_id_type=MESH)

    def vol_copy(t):
        return pltpu.make_async_remote_copy(
            src_ref=vpack.at[0], dst_ref=vpack.at[t], send_sem=vs_sem.at[t], recv_sem=vr_sem.at[t],
            device_id={"ctl": lax.rem(my_c + nc - t, nc)}, device_id_type=MESH)

    def weight_copy(s):
        return pltpu.make_async_remote_copy(
            src_ref=wsend.at[s], dst_ref=wrecv.at[s], send_sem=ws_sem.at[s], recv_sem=wr_sem.at[s],
            device_id={"vol": lax.rem(my_v + s, nv)}, device_id_type=MESH)

    def part_copy(t):
        return pltpu.make_async_remote_copy(
            src_ref=psend.at[t], dst_ref=precv.at[t], send_sem=ps_sem.at[t], recv_sem=pr_sem.at[t],
            device_id={"ctl": lax.rem(my_c + t, nc)}, device_id_type=MESH)

    for s in range(1, nv):
        ctl_copy(s).start()
    for t in range(1, nc):
        vol_copy(t).start()

    wacc[...] = jnp.zeros_like(wacc)
    cacc[...] = jnp.zeros_like(cacc)
    rhs[...] = jnp.zeros_like(rhs)

    def make_rhs(s):
        rhs[s, :rows, :own_c] = cpack[s, :rows]
        aug = cpack[s, rows:].astype(jnp.float32)
        row = lax.broadcasted_iota(jnp.int32, aug.shape, 0)
        aug = jnp.where(row < 3, -2.0 * inverse_square * aug, aug)
        rhs[s, rows:, own_c:] = aug.astype(jnp.bfloat16)

    chunk = math.gcd(own_v, 64)

    def tile(t, s):
        kernels, weightings = [], []
        for r in range(0, own_v, chunk):
            both = jnp.dot(vt[t, r : r + chunk], rhs[s], preferred_element_type=jnp.float32)
            square = jnp.maximum(both[:, own_c:], 1e-30)
            inside = jnp.maximum(1.0 - square * lax.rsqrt(square), 0.0)
            second = inside * inside
            kernels.append((second * second * (5.0 - 4.0 * inside)).astype(jnp.bfloat16))
            weightings.append((second * inside * both[:, :own_c]).astype(jnp.bfloat16))
        kern = jnp.concatenate(kernels, axis=0)
        weighting = jnp.concatenate(weightings, axis=0)
        wacc[s] += jnp.dot(vpack[t, :rows], kern, preferred_element_type=jnp.float32)
        cacc[s] += jnp.dot(vpack[t, rows:], weighting, preferred_element_type=jnp.float32)
        return lax.dot_general(
            cpack[s, rows:], weighting, (((1,), (1,)), ((), ())), preferred_element_type=jnp.float32)

    def turn(t):
        vt[t] = vpack[t].astype(jnp.float32).T.astype(jnp.bfloat16)

    def part(t, pulled):
        pos = vpack[t, rows:].astype(jnp.float32)[:8]
        psend[t] = slope_factor * (pos * pulled[3:4] - pulled[:8])

    group = math.gcd(nv, 4)

    turn(0)
    make_rhs(0)
    pulled = tile(0, 0)
    if nv <= 4:
        for s in range(1, nv):
            ctl_copy(s).wait_recv()
            make_rhs(s)
            pulled += tile(0, s)
    else:
        def first(s, total):
            ctl_copy(s).wait_recv()
            make_rhs(s)
            return total + tile(0, s)
        pulled = lax.fori_loop(1, nv, first, pulled)
    part(0, pulled)

    def volume_step(t, carry):
        vol_copy(t).wait_recv()
        turn(t)

        def some(g, total):
            for k in range(group):
                total += tile(t, g * group + k)
            return total

        zero = jnp.zeros((AUG, own_v), jnp.float32)
        total = some(0, zero) if nv == group else lax.fori_loop(0, nv // group, some, zero)
        part(t, total)
        part_copy(t).start()
        return carry

    lax.fori_loop(1, nc, volume_step, 0)

    def message(s):
        pos = cpack[s, rows:].astype(jnp.float32)[:8]
        wsend[s, :rows] = wacc[s]
        wsend[s, rows:] = slope_factor * (pos * cacc[s, 6:7] - cacc[s, :8])

    for s in range(1, nv):
        message(s)
        weight_copy(s).start()
    message(0)

    total = psend[0]
    for t in range(1, nc):
        part_copy(t).wait_recv()
        total += precv[t]
    out_v[...] = total[:3]
    total = wsend[0]
    for s in range(1, nv):
        weight_copy(s).wait_recv()
        total += wrecv[s]
    out_w[...] = total[:rows]
    out_c[...] = total[rows : rows + 3]

    for s in range(1, nv):
        ctl_copy(s).wait_send()
        weight_copy(s).wait_send()
    for t in range(1, nc):
        vol_copy(t).wait_send()
        part_copy(t).wait_send()


def shards(nv, nc, vol_coords, vol_cotangent, ctl_coords, ctl_weights):
    rows, own_v = vol_cotangent.shape
    own_c = ctl_weights.shape[1]
    depth = rows + AUG
    vmem = pl.BlockSpec(memory_space=pltpu.VMEM)
    f32, bf16 = jnp.float32, jnp.bfloat16
    dma = pltpu.SemaphoreType.DMA
    return pl.pallas_call(
        functools.partial(kernel, nv, nc),
        out_shape=(
            jax.ShapeDtypeStruct((rows, own_c), f32),
            jax.ShapeDtypeStruct((3, own_v), f32),
            jax.ShapeDtypeStruct((3, own_c), f32),
        ),
        in_specs=[vmem] * 4,
        out_specs=(vmem,) * 3,
        scratch_shapes=[
            pltpu.VMEM((nc, depth, own_v), bf16),
            pltpu.VMEM((nv, depth, own_c), bf16),
            pltpu.VMEM((nc, own_v, depth), bf16),
            pltpu.VMEM((nv, depth, 2 * own_c), bf16),
            pltpu.VMEM((nv, rows, own_c), f32),
            pltpu.VMEM((nv, AUG, own_c), f32),
            pltpu.VMEM((nv, rows + 8, own_c), f32),
            pltpu.VMEM((nv, rows + 8, own_c), f32),
            pltpu.VMEM((nc, 8, own_v), f32),
            pltpu.VMEM((nc, 8, own_v), f32),
            dma((nc,)), dma((nc,)), dma((nv,)), dma((nv,)),
            dma((nv,)), dma((nv,)), dma((nc,)), dma((nc,)),
        ],
        compiler_params=pltpu.CompilerParams(collective_id=0, has_side_effects=True),
    )(vol_coords, vol_cotangent, ctl_coords, ctl_weights)


def solution(mesh):
    in_specs = (
        P(None, ("vol", "ctl")),
        P(None, ("vol", "ctl")),
        P(None, ("ctl", "vol")),
        P(None, ("ctl", "vol")),
    )
    out_specs = (P(None, ("ctl", "vol")), P(None, ("vol", "ctl")), P(None, ("ctl", "vol")))
    body = functools.partial(shards, mesh.shape["vol"], mesh.shape["ctl"])
    return jax.shard_map(body, mesh=mesh, in_specs=in_specs, out_specs=out_specs, check_vma=False)
```

```python
import functools
import math

import jax
import jax.numpy as jnp
from jax import lax
from jax.experimental import pallas as pl
from jax.experimental.pallas import tpu as pltpu
from jax.sharding import PartitionSpec as P

MESH = pl.DeviceIdType.MESH
slope_factor = -20.0 / (0.25 * 0.25)
inverse_square = 256.0
EARLY = 4
AUG = 16


def augment(dst, slot, coords_ref, values_ref, norm_row, ones_row):
    rows = values_ref.shape[0]
    dst[slot, :rows] = values_ref[...]
    pos = coords_ref[...].astype(jnp.float32)
    x, y, z = pos[0:1], pos[1:2], pos[2:3]
    norm = inverse_square * (x * x + y * y + z * z)
    high = norm.astype(jnp.bfloat16).astype(jnp.float32)
    rest = norm - high
    middle = rest.astype(jnp.bfloat16).astype(jnp.float32)
    low = rest - middle
    row = lax.broadcasted_iota(jnp.int32, (AUG, pos.shape[1]), 0)
    aug = jnp.where((row >= ones_row) & (row < ones_row + 3), 1.0, 0.0)
    pieces = ((0, x), (1, y), (2, z), (norm_row, high), (norm_row + 1, middle), (norm_row + 2, low))
    for at, piece in pieces:
        aug = jnp.where(row == at, piece, aug)
    dst[slot, rows:] = aug.astype(jnp.bfloat16)


def kernel(
    nv, nc, vxyz, vcot, cxyz, cwts, out_w, out_v, out_c,
    vpack, cpack, vt, rhs, wacc, cacc, vacc, wsend, wrecv, psend, precv,
    vs_sem, vr_sem, cs_sem, cr_sem, ws_sem, wr_sem, ps_sem, pr_sem,
):
    rows, own_v = vcot.shape
    own_c = cwts.shape[1]
    my_v, my_c = lax.axis_index("vol"), lax.axis_index("ctl")
    near = math.gcd(nv, 2)

    def partner(s, sign):
        outer = lax.rem(my_v // near + nv // near + sign * (s // near), nv // near)
        return outer * near + lax.rem(lax.rem(my_v, near) + near + sign * (s % near), near)

    pair = math.gcd(nc, 2)
    line = nc // pair
    at = my_c // pair
    from_low = at * 2 < line
    edge = jnp.where(from_low, at, line - 1 - at)

    def visit(k):
        step = k // pair
        swing = jnp.where(lax.rem(step, 2) == 1, edge - (step + 1) // 2, edge + step // 2)
        place = jnp.where(step <= 2 * edge, swing, step)
        place = jnp.where(from_low, place, line - 1 - place)
        return place * pair + lax.rem(lax.rem(my_c, pair) + lax.rem(k, pair), pair)

    barrier = pltpu.get_barrier_semaphore()
    for s in range(1, nv):
        pl.semaphore_signal(barrier, inc=1, device_id={"vol": partner(s, 1)}, device_id_type=MESH)
    for t in range(1, nc):
        pl.semaphore_signal(barrier, inc=1, device_id={"ctl": lax.rem(my_c + t, nc)}, device_id_type=MESH)

    def ctl_copy(s):
        return pltpu.make_async_remote_copy(
            src_ref=cpack.at[0], dst_ref=cpack.at[s], send_sem=cs_sem.at[s], recv_sem=cr_sem.at[s],
            device_id={"vol": partner(s, -1)}, device_id_type=MESH)

    def vol_copy(to, slot):
        return pltpu.make_async_remote_copy(
            src_ref=vpack.at[my_c], dst_ref=vpack.at[slot], send_sem=vs_sem.at[to], recv_sem=vr_sem.at[slot],
            device_id={"ctl": to}, device_id_type=MESH)

    def weight_copy(s):
        return pltpu.make_async_remote_copy(
            src_ref=wsend.at[s], dst_ref=wrecv.at[s], send_sem=ws_sem.at[s], recv_sem=wr_sem.at[s],
            device_id={"vol": partner(s, 1)}, device_id_type=MESH)

    def part_copy(to, slot):
        return pltpu.make_async_remote_copy(
            src_ref=psend.at[to], dst_ref=precv.at[slot], send_sem=ps_sem.at[to], recv_sem=pr_sem.at[slot],
            device_id={"ctl": to}, device_id_type=MESH)

    augment(vpack, my_c, vxyz, vcot, 3, 6)
    augment(cpack, 0, cxyz, cwts, 6, 3)
    wacc[...] = jnp.zeros_like(wacc)
    cacc[...] = jnp.zeros_like(cacc)
    rhs[...] = jnp.zeros_like(rhs)

    def make_rhs(s):
        rhs[s, :rows, :own_c] = cpack[s, :rows]
        aug = cpack[s, rows:].astype(jnp.float32)
        row = lax.broadcasted_iota(jnp.int32, aug.shape, 0)
        aug = jnp.where(row < 3, -2.0 * inverse_square * aug, aug)
        rhs[s, rows:, own_c:] = aug.astype(jnp.bfloat16)

    chunk = math.gcd(own_v, 64)

    def tile(t, s):
        kernels, weightings = [], []
        for r in range(0, own_v, chunk):
            both = jnp.dot(vt[t, r : r + chunk], rhs[s], preferred_element_type=jnp.float32)
            square = jnp.maximum(both[:, own_c:], 1e-30)
            inside = jnp.maximum(4.0 - square * lax.rsqrt(square), 0.0)
            second = inside * inside
            kernels.append((second * second * (5.0 - inside)).astype(jnp.bfloat16))
            weightings.append((second * inside * both[:, :own_c]).astype(jnp.bfloat16))
        kern = jnp.concatenate(kernels, axis=0)
        weighting = jnp.concatenate(weightings, axis=0)
        wacc[s] += jnp.dot(vpack[t, :rows], kern, preferred_element_type=jnp.float32)
        cacc[s] += jnp.dot(vpack[t, rows:], weighting, preferred_element_type=jnp.float32)
        return lax.dot_general(
            cpack[s, rows:], weighting, (((1,), (1,)), ((), ())), preferred_element_type=jnp.float32)

    def turn(t):
        vt[t] = vpack[t].astype(jnp.float32).T.astype(jnp.bfloat16)

    def part(t, pulled):
        pos = vpack[t, rows:].astype(jnp.float32)[:8]
        psend[t] = (slope_factor / 64.0) * (pos * pulled[3:4] - pulled[:8])

    def tiles(t, first, last, total):
        count = last - first
        group = math.gcd(count, 4)
        if count <= 4:
            for s in range(first, last):
                total += tile(t, s)
            return total

        def some(g, running):
            for k in range(group):
                running += tile(t, first + g * group + k)
            return running

        return lax.fori_loop(0, count // group, some, total)

    def message(s):
        pos = cpack[s, rows:].astype(jnp.float32)[:8]
        wsend[s, :rows] = wacc[s] * (1.0 / 256.0)
        wsend[s, rows:] = (slope_factor / 64.0) * (pos * cacc[s, 6:7] - cacc[s, :8])

    turn(my_c)
    make_rhs(0)
    pulled = tile(my_c, 0)
    pl.semaphore_wait(barrier, nv + nc - 2)
    for s in range(1, nv):
        ctl_copy(s).start()
    for k in range(1, nc):
        vol_copy(visit(k), my_c).start()

    def first(s, total):
        ctl_copy(s).wait_recv()
        make_rhs(s)
        return total + tile(my_c, s)

    if nv <= 4:
        for s in range(1, nv):
            pulled = first(s, pulled)
    else:
        pulled = lax.fori_loop(1, nv, first, pulled)
    part(my_c, pulled)

    zero = jnp.zeros((AUG, own_v), jnp.float32)
    early = min(EARLY, nc)

    def arrive(t):
        vol_copy(t, t).wait_recv()
        turn(t)

    def whole_step(k, carry):
        t = visit(k)
        arrive(t)
        part(t, tiles(t, 0, nv, zero))
        part_copy(t, my_c).start()
        return carry

    def outer_step(k, carry):
        t = visit(k)
        arrive(t)
        vacc[t] = tiles(t, near, nv, zero)
        return carry

    def inner_step(k, carry):
        t = visit(nc - 1 - k)
        part(t, tiles(t, 0, near, vacc[t]))
        part_copy(t, my_c).start()
        return carry

    lax.fori_loop(1, early, whole_step, 0)
    lax.fori_loop(early, nc, outer_step, 0)
    for s in range(near, nv):
        message(s)
        weight_copy(s).start()
    lax.fori_loop(0, nc - early, inner_step, 0)
    for s in range(1, near):
        message(s)
        weight_copy(s).start()
    message(0)

    total = psend[my_c]
    for t in range(1, nc):
        slot = lax.rem(my_c + t, nc)
        part_copy(slot, slot).wait_recv()
        total += precv[slot]
    out_v[...] = total[:3]
    total = wsend[0]
    for s in range(nv - 1, 0, -1):
        weight_copy(s).wait_recv()
        total += wrecv[s]
    out_w[...] = total[:rows]
    out_c[...] = total[rows : rows + 3]

    for s in range(1, nv):
        ctl_copy(s).wait_send()
        weight_copy(s).wait_send()
    for t in range(1, nc):
        slot = lax.rem(my_c + t, nc)
        vol_copy(slot, slot).wait_send()
        part_copy(slot, slot).wait_send()


def shards(nv, nc, vol_coords, vol_cotangent, ctl_coords, ctl_weights):
    rows, own_v = vol_cotangent.shape
    own_c = ctl_weights.shape[1]
    depth = rows + AUG
    vmem = pl.BlockSpec(memory_space=pltpu.VMEM)
    f32, bf16 = jnp.float32, jnp.bfloat16
    dma = pltpu.SemaphoreType.DMA
    shapes = ((rows, own_c), (3, own_v), (3, own_c))
    held = pl.pallas_call(
        functools.partial(kernel, nv, nc),
        out_shape=tuple(pltpu.VMEM(shape, f32) for shape in shapes),
        in_specs=[vmem] * 4,
        out_specs=(vmem,) * 3,
        scratch_shapes=[
            pltpu.VMEM((nc, depth, own_v), bf16),
            pltpu.VMEM((nv, depth, own_c), bf16),
            pltpu.VMEM((nc, own_v, depth), bf16),
            pltpu.VMEM((nv, depth, 2 * own_c), bf16),
            pltpu.VMEM((nv, rows, own_c), f32),
            pltpu.VMEM((nv, AUG, own_c), f32),
            pltpu.VMEM((nc, AUG, own_v), f32),
            pltpu.VMEM((nv, rows + 8, own_c), f32),
            pltpu.VMEM((nv, rows + 8, own_c), f32),
            pltpu.VMEM((nc, 8, own_v), f32),
            pltpu.VMEM((nc, 8, own_v), f32),
            dma((nc,)), dma((nc,)), dma((nv,)), dma((nv,)),
            dma((nv,)), dma((nv,)), dma((nc,)), dma((nc,)),
        ],
        compiler_params=pltpu.CompilerParams(collective_id=0, has_side_effects=True),
    )(vol_coords, vol_cotangent, ctl_coords, ctl_weights)
    return held


def solution(mesh):
    in_specs = (
        P(None, ("vol", "ctl")),
        P(None, ("vol", "ctl")),
        P(None, ("ctl", "vol")),
        P(None, ("ctl", "vol")),
    )
    out_specs = (P(None, ("ctl", "vol")), P(None, ("vol", "ctl")), P(None, ("ctl", "vol")))
    body = functools.partial(shards, mesh.shape["vol"], mesh.shape["ctl"])
    return jax.shard_map(body, mesh=mesh, in_specs=in_specs, out_specs=out_specs, check_vma=False)
```

```python
import functools
import math

import jax
import jax.numpy as jnp
from jax import lax
from jax.experimental import pallas as pl
from jax.experimental.pallas import tpu as pltpu
from jax.sharding import PartitionSpec as P

MESH = pl.DeviceIdType.MESH
slope_factor = -20.0 / (0.25 * 0.25)
inverse_square = 256.0
EARLY = 4
AUG = 16


def augment(dst, slot, coords_ref, rows, norm_row, ones_row):
    pos = coords_ref[...].astype(jnp.float32)
    x, y, z = pos[0:1], pos[1:2], pos[2:3]
    norm = inverse_square * (x * x + y * y + z * z)
    high = norm.astype(jnp.bfloat16).astype(jnp.float32)
    rest = norm - high
    middle = rest.astype(jnp.bfloat16).astype(jnp.float32)
    low = rest - middle
    row = lax.broadcasted_iota(jnp.int32, (AUG, pos.shape[1]), 0)
    aug = jnp.where((row >= ones_row) & (row < ones_row + 3), 1.0, 0.0)
    pieces = ((0, x), (1, y), (2, z), (norm_row, high), (norm_row + 1, middle), (norm_row + 2, low))
    for at, piece in pieces:
        aug = jnp.where(row == at, piece, aug)
    dst[slot, rows:] = aug.astype(jnp.bfloat16)


def kernel(
    nv, nc, vxyz, vcot, cxyz, cwts, out_w, out_v, out_c, vpos, cpos,
    vpack, cpack, vt, rhs, wacc, cacc, vacc, wsend, wrecv, psend, precv,
    vs_sem, vr_sem, cs_sem, cr_sem, ws_sem, wr_sem, ps_sem, pr_sem, load_sem,
):
    rows, own_v = vcot.shape
    own_c = cwts.shape[1]
    my_v, my_c = lax.axis_index("vol"), lax.axis_index("ctl")
    near = math.gcd(nv, 2)

    def partner(s, sign):
        outer = lax.rem(my_v // near + nv // near + sign * (s // near), nv // near)
        return outer * near + lax.rem(lax.rem(my_v, near) + near + sign * (s % near), near)

    pair = math.gcd(nc, 2)
    line = nc // pair
    at = my_c // pair
    from_low = at * 2 < line
    edge = jnp.where(from_low, at, line - 1 - at)

    def visit(k):
        step = k // pair
        swing = jnp.where(lax.rem(step, 2) == 1, edge - (step + 1) // 2, edge + step // 2)
        place = jnp.where(step <= 2 * edge, swing, step)
        place = jnp.where(from_low, place, line - 1 - place)
        return place * pair + lax.rem(lax.rem(my_c, pair) + lax.rem(k, pair), pair)

    barrier = pltpu.get_barrier_semaphore()
    for s in range(1, nv):
        pl.semaphore_signal(barrier, inc=1, device_id={"vol": partner(s, 1)}, device_id_type=MESH)
    for t in range(1, nc):
        pl.semaphore_signal(barrier, inc=1, device_id={"ctl": lax.rem(my_c + t, nc)}, device_id_type=MESH)

    def ctl_copy(s):
        return pltpu.make_async_remote_copy(
            src_ref=cpack.at[0], dst_ref=cpack.at[s], send_sem=cs_sem.at[s], recv_sem=cr_sem.at[s],
            device_id={"vol": partner(s, -1)}, device_id_type=MESH)

    def vol_copy(to, slot):
        return pltpu.make_async_remote_copy(
            src_ref=vpack.at[my_c], dst_ref=vpack.at[slot], send_sem=vs_sem.at[to], recv_sem=vr_sem.at[slot],
            device_id={"ctl": to}, device_id_type=MESH)

    def weight_copy(s):
        return pltpu.make_async_remote_copy(
            src_ref=wsend.at[s], dst_ref=wrecv.at[s], send_sem=ws_sem.at[s], recv_sem=wr_sem.at[s],
            device_id={"vol": partner(s, 1)}, device_id_type=MESH)

    def part_copy(to, slot):
        return pltpu.make_async_remote_copy(
            src_ref=psend.at[to], dst_ref=precv.at[slot], send_sem=ps_sem.at[to], recv_sem=pr_sem.at[slot],
            device_id={"ctl": to}, device_id_type=MESH)

    loads = [
        pltpu.make_async_copy(src, dst, load_sem.at[k])
        for k, (src, dst) in enumerate((
            (vxyz, vpos), (cxyz, cpos), (cwts, cpack.at[0, pl.ds(0, rows)]), (vcot, vpack.at[my_c, pl.ds(0, rows)])))
    ]
    for load in loads:
        load.start()
    for load in loads:
        load.wait()
    augment(vpack, my_c, vpos, rows, 3, 6)
    augment(cpack, 0, cpos, rows, 6, 3)
    wacc[...] = jnp.zeros_like(wacc)
    cacc[...] = jnp.zeros_like(cacc)
    rhs[...] = jnp.zeros_like(rhs)

    def make_rhs(s):
        rhs[s, :rows, :own_c] = cpack[s, :rows]
        aug = cpack[s, rows:].astype(jnp.float32)
        row = lax.broadcasted_iota(jnp.int32, aug.shape, 0)
        aug = jnp.where(row < 3, -2.0 * inverse_square * aug, aug)
        rhs[s, rows:, own_c:] = aug.astype(jnp.bfloat16)

    chunk = math.gcd(own_v, 64)

    def tile(t, s):
        kernels, weightings = [], []
        for r in range(0, own_v, chunk):
            both = jnp.dot(vt[t, r : r + chunk], rhs[s], preferred_element_type=jnp.float32)
            square = jnp.maximum(both[:, own_c:], 1e-30)
            inside = jnp.maximum(4.0 - square * lax.rsqrt(square), 0.0)
            second = inside * inside
            kernels.append((second * second * (5.0 - inside)).astype(jnp.bfloat16))
            weightings.append((second * inside * both[:, :own_c]).astype(jnp.bfloat16))
        kern = jnp.concatenate(kernels, axis=0)
        weighting = jnp.concatenate(weightings, axis=0)
        wacc[s] += jnp.dot(vpack[t, :rows], kern, preferred_element_type=jnp.float32)
        cacc[s] += jnp.dot(vpack[t, rows:], weighting, preferred_element_type=jnp.float32)
        return lax.dot_general(
            cpack[s, rows:], weighting, (((1,), (1,)), ((), ())), preferred_element_type=jnp.float32)

    def turn(t):
        vt[t] = vpack[t].astype(jnp.float32).T.astype(jnp.bfloat16)

    def part(t, pulled):
        pos = vpack[t, rows:].astype(jnp.float32)[:8]
        psend[t] = (slope_factor / 64.0) * (pos * pulled[3:4] - pulled[:8])

    def tiles(t, first, last, total):
        count = last - first
        group = math.gcd(count, 4)
        if count <= 4:
            for s in range(first, last):
                total += tile(t, s)
            return total

        def some(g, running):
            for k in range(group):
                running += tile(t, first + g * group + k)
            return running

        return lax.fori_loop(0, count // group, some, total)

    def message(s):
        pos = cpack[s, rows:].astype(jnp.float32)[:8]
        wsend[s, :rows] = wacc[s] * (1.0 / 256.0)
        wsend[s, rows:] = (slope_factor / 64.0) * (pos * cacc[s, 6:7] - cacc[s, :8])

    turn(my_c)
    make_rhs(0)
    pulled = tile(my_c, 0)
    pl.semaphore_wait(barrier, nv + nc - 2)
    for s in range(1, nv):
        ctl_copy(s).start()
    for k in range(1, nc):
        vol_copy(visit(k), my_c).start()

    def first(s, total):
        ctl_copy(s).wait_recv()
        make_rhs(s)
        return total + tile(my_c, s)

    if nv <= 4:
        for s in range(1, nv):
            pulled = first(s, pulled)
    else:
        pulled = lax.fori_loop(1, nv, first, pulled)
    part(my_c, pulled)

    zero = jnp.zeros((AUG, own_v), jnp.float32)
    early = min(EARLY, nc)

    def arrive(t):
        vol_copy(t, t).wait_recv()
        turn(t)

    def whole_step(k, carry):
        t = visit(k)
        arrive(t)
        part(t, tiles(t, 0, nv, zero))
        part_copy(t, my_c).start()
        return carry

    def outer_step(k, carry):
        t = visit(k)
        arrive(t)
        vacc[t] = tiles(t, near, nv, zero)
        return carry

    def inner_step(k, carry):
        t = visit(nc - 1 - k)
        part(t, tiles(t, 0, near, vacc[t]))
        part_copy(t, my_c).start()
        return carry

    lax.fori_loop(1, early, whole_step, 0)
    lax.fori_loop(early, nc, outer_step, 0)
    for s in range(near, nv):
        message(s)
        weight_copy(s).start()
    lax.fori_loop(0, nc - early, inner_step, 0)
    for s in range(1, near):
        message(s)
        weight_copy(s).start()
    message(0)

    total = psend[my_c]
    for t in range(1, nc):
        slot = lax.rem(my_c + t, nc)
        part_copy(slot, slot).wait_recv()
        total += precv[slot]
    out_v[...] = total[:3]
    total = wsend[0]
    for s in range(nv - 1, 0, -1):
        weight_copy(s).wait_recv()
        total += wrecv[s]
    out_w[...] = total[:rows]
    out_c[...] = total[rows : rows + 3]

    for s in range(1, nv):
        ctl_copy(s).wait_send()
        weight_copy(s).wait_send()
    for t in range(1, nc):
        slot = lax.rem(my_c + t, nc)
        vol_copy(slot, slot).wait_send()
        part_copy(slot, slot).wait_send()


def shards(nv, nc, vol_coords, vol_cotangent, ctl_coords, ctl_weights):
    rows, own_v = vol_cotangent.shape
    own_c = ctl_weights.shape[1]
    depth = rows + AUG
    vmem = pl.BlockSpec(memory_space=pltpu.VMEM)
    f32, bf16 = jnp.float32, jnp.bfloat16
    dma = pltpu.SemaphoreType.DMA
    shapes = ((rows, own_c), (3, own_v), (3, own_c))
    held = pl.pallas_call(
        functools.partial(kernel, nv, nc),
        out_shape=tuple(pltpu.VMEM(shape, f32) for shape in shapes),
        in_specs=[pl.BlockSpec(memory_space=pl.ANY)] * 4,
        out_specs=(vmem,) * 3,
        scratch_shapes=[
            pltpu.VMEM((3, own_v), bf16),
            pltpu.VMEM((3, own_c), bf16),
            pltpu.VMEM((nc, depth, own_v), bf16),
            pltpu.VMEM((nv, depth, own_c), bf16),
            pltpu.VMEM((nc, own_v, depth), bf16),
            pltpu.VMEM((nv, depth, 2 * own_c), bf16),
            pltpu.VMEM((nv, rows, own_c), f32),
            pltpu.VMEM((nv, AUG, own_c), f32),
            pltpu.VMEM((nc, AUG, own_v), f32),
            pltpu.VMEM((nv, rows + 8, own_c), f32),
            pltpu.VMEM((nv, rows + 8, own_c), f32),
            pltpu.VMEM((nc, 8, own_v), f32),
            pltpu.VMEM((nc, 8, own_v), f32),
            dma((nc,)), dma((nc,)), dma((nv,)), dma((nv,)),
            dma((nv,)), dma((nv,)), dma((nc,)), dma((nc,)), dma((4,)),
        ],
        compiler_params=pltpu.CompilerParams(collective_id=0, has_side_effects=True),
    )(vol_coords, vol_cotangent, ctl_coords, ctl_weights)
    return held


def solution(mesh):
    in_specs = (
        P(None, ("vol", "ctl")),
        P(None, ("vol", "ctl")),
        P(None, ("ctl", "vol")),
        P(None, ("ctl", "vol")),
    )
    out_specs = (P(None, ("ctl", "vol")), P(None, ("vol", "ctl")), P(None, ("ctl", "vol")))
    body = functools.partial(shards, mesh.shape["vol"], mesh.shape["ctl"])
    return jax.shard_map(body, mesh=mesh, in_specs=in_specs, out_specs=out_specs, check_vma=False)
```
